32 devices in a mesh: ia: 2 (over y), ja: 4 (over z), ka: 4 (over x, core).
Axes of the slice: x: 2, y: 2, z: 4, core: 2. Of those that a mesh axis runs over, the one named last changes fastest.
Arguments:
- blocks: bfloat16 [256, 64, 4096], P(('ia', 'ja', 'ka')), may hold values from -12 to 12
- coords: int32 [256, 3], P(('ia', 'ja', 'ka')), may hold values from 0 to 63, as said below
- factor_one: float32 [2048, 512], P('ia'), may hold values from -1.2 to 1.2
- factor_two: float32 [4096, 512], P('ja'), may hold values from -1.2 to 1.2
- factor_three: float32 [4096, 512], P('ka'), may hold values from -1.2 to 1.2
Outputs:
- swept_one: float32 [2048, 512], P('ia')
- swept_two: float32 [4096, 512], P('ja')
- swept_three: float32 [4096, 512], P('ka')
The draws below stay inside these ranges and needn't reach their ends.
Inputs may be any that keep to these rules, and one draw needn't show every extreme that they name: Row n of coords holds the three block coordinates of block n. The 8 rows of one device of ia+ja+ka (aligned blocks of 8 rows, devices in the order ia, ja, ka) have their second coordinate within that device's ja range (16 * ja to 16 * ja + 15) and their third within its ka range; at most 8 of them have a first coordinate within any one index of ia's range of 16; in every group of devices that share ja and ka, some index of ia receives exactly 8 from each device of the group. The same block may be listed more than once.
All inputs are finite; a program needn't handle non-finite values.
Results may differ from the reference program's by a relative error of at most 0.0028.
Values may be sent and summed in bfloat16 or wider, within the bound.
A program may use at most 64 MiB of HBM per device.

```python
import jax
import jax.numpy as jnp
from jax import lax

B = 64
R = 512
BR = 16
BLK_DEV = 8
CAP = 8
NBLK = 256
I = 2048
J = 4096
K = 4096
N_IA = 2
N_JA = 4
N_KA = 4
DEVICES = 32


def draw_coords(key, part):
    pool = N_IA * CAP

    def one_source(device):
        own = jax.random.fold_in(key, device)
        column = device % (N_JA * N_KA)
        crowded = jax.random.randint(jax.random.fold_in(key, DEVICES + column), (), 0, N_IA)
        order = jax.random.permutation(jax.random.fold_in(own, 1), pool)
        score = jnp.where(order // CAP == crowded, order - pool, jnp.arange(pool))
        chosen = order[jnp.argsort(score, stable=True)][:BLK_DEV]
        target = chosen // CAP
        offsets = jax.random.randint(jax.random.fold_in(own, 2), (BLK_DEV, 3), 0, BR)
        second = jnp.full((BLK_DEV,), device // N_KA % N_JA)
        third = jnp.full((BLK_DEV,), device % N_KA)
        lower = jnp.stack([target, second, third], axis=1)
        return (lower * BR + offsets).astype(jnp.int32)
    listed = jax.vmap(one_source)(jnp.arange(DEVICES))
    return listed.reshape(DEVICES * BLK_DEV, 3)


def block_levels(own_key, shape, shards, least, high):
    level = 1.0
    for axis_at, parts in shards:
        draws = jax.random.uniform(jax.random.fold_in(jax.random.fold_in(own_key, 6), axis_at), (parts,), jnp.float32, least / len(shards), high / len(shards))
        level = level * jnp.repeat(jnp.exp(draws), shape[axis_at] // parts).reshape((-1,) + (1,) * (len(shape) - 1 - axis_at))
    return level


def noise(own_key, extent, deviation, reach, split=(), dtype=jnp.bfloat16):
    entries = jax.random.normal(own_key, extent, jnp.float32) * deviation
    if len(split) > 0:
        entries = block_levels(own_key, extent, split, -0.22, 0.18) * entries
    return jnp.clip(entries, min=-reach, max=reach).astype(dtype)


def setup_inputs(seed: int = 0) -> dict:
    streams_of = jax.random.split(jax.random.key(seed), 6)
    blocks = noise(streams_of[0], (NBLK, B, B * B), 2.0, 12.0, ((0, 32),))
    coords = draw_coords(jax.random.fold_in(streams_of[5], 71), 0)
    factor_one = noise(streams_of[2], (I, R), 0.2, 1.2, ((0, 2),), jnp.float32)
    factor_two = noise(streams_of[3], (J, R), 0.2, 1.2, ((0, 4),), jnp.float32)
    factor_three = noise(streams_of[4], (K, R), 0.2, 1.2, ((0, 4),), jnp.float32)
    return {"blocks": blocks, "coords": coords, "factor_one": factor_one, "factor_two": factor_two, "factor_three": factor_three}


STEP_SIZE = 0.01
einsum_forms = (("qk,rk->qrk", "pk,qrk->pqr", "pqr,qrk->pk"),
                ("pk,rk->prk", "qk,prk->pqr", "pqr,prk->qk"),
                ("pk,qk->pqk", "rk,pqk->pqr", "pqr,pqk->rk"))
other_modes = ((1, 2), (0, 2), (0, 1))


def block_gradient(cube, rows, mode):
    first, second = other_modes[mode]
    outer_form, model_form, grad_form = einsum_forms[mode]
    khatri = jnp.einsum(outer_form, rows[first].astype(jnp.float32), rows[second].astype(jnp.float32)).astype(jnp.bfloat16)
    model = jnp.einsum(model_form, rows[mode].astype(jnp.float32), khatri.astype(jnp.float32))
    misfit = (cube.astype(jnp.float32) - model).astype(jnp.bfloat16)
    return jnp.einsum(grad_form, misfit.astype(jnp.float32), khatri.astype(jnp.float32))


def mode_gradient(blocks, coords, rounded, mode, shape):
    def visit(total, item):
        cube, place = item
        rows = tuple(lax.dynamic_slice_in_dim(rounded[f], place[f] * B, B, 0) for f in range(3))
        term = block_gradient(cube.reshape(B, B, B), rows, mode)
        offset = place[mode] * B
        current = lax.dynamic_slice_in_dim(total, offset, B, 0)
        return lax.dynamic_update_slice_in_dim(total, current + term, offset, 0), None

    return lax.scan(visit, jnp.zeros(shape, jnp.float32), (blocks, coords))[0]


def reference(blocks, coords, factor_one, factor_two, factor_three):
    factors = [factor_one, factor_two, factor_three]
    for mode in range(3):
        rounded = tuple(f.astype(jnp.bfloat16) for f in factors)
        total = mode_gradient(blocks, coords, rounded, mode, factors[mode].shape)
        factors[mode] = factors[mode] + STEP_SIZE * total
    return factors[0], factors[1], factors[2]
```

```python
import functools

import jax
import jax.numpy as jnp
from jax import lax
from jax.experimental import pallas as pl
from jax.experimental.pallas import tpu as pltpu
from jax.sharding import PartitionSpec as P

STEP_SIZE = 0.01
F32 = jnp.float32
BF16 = jnp.bfloat16


def gradient_kernel(mode, group, place_ref, x_ref, one_ref, two_ref, three_ref, out_ref, acc, term, three_pad):
    step = pl.program_id(0)
    edge, width = one_ref.shape
    lanes = group * edge

    @pl.when(step == 0)
    def _():
        acc[...] = jnp.zeros_like(acc)

    one = one_ref[...].astype(BF16)
    two = two_ref[...].astype(BF16)
    three = three_ref[...].astype(BF16)
    two_wide = two.astype(F32)
    if mode == 1:
        one_wide = one.astype(F32)
        three_pad[...] = jnp.zeros_like(three_pad)
        three_pad[0, :edge, :] = three
        three_pad[1, edge:, :] = three
    else:
        term[...] = jnp.zeros_like(term)
    for c in range(edge // group):
        kr = jnp.concatenate(
            [
                jnp.broadcast_to(two_wide[q : q + 1, :], (edge, width)).astype(BF16) * three
                for q in range(c * group, (c + 1) * group)
            ],
            axis=0,
        )
        model = lax.dot_general(one, kr, (((1,), (1,)), ((), ())), preferred_element_type=F32)
        misfit = (x_ref[0, :, c * lanes : (c + 1) * lanes].astype(F32) - model).astype(BF16)
        if mode == 0:
            term[...] += jnp.dot(misfit, kr, preferred_element_type=F32)
        elif mode == 1:
            for pair in range(group // 2):
                both = misfit[:, pair * 2 * edge : (pair + 1) * 2 * edge]
                for half in range(2):
                    mixed = jnp.dot(both, three_pad[half], preferred_element_type=F32)
                    q = c * group + 2 * pair + half
                    term[q : q + 1, :] = jnp.sum(mixed * one_wide, axis=0, keepdims=True)
        else:
            mixed = lax.dot_general(misfit, one, (((0,), (0,)), ((), ())), preferred_element_type=F32)
            total = None
            for g in range(group):
                q = c * group + g
                part = mixed[g * edge : (g + 1) * edge, :] * two_wide[q : q + 1, :]
                total = part if total is None else total + part
            term[...] += total
    offset = pl.multiple_of(place_ref[step, mode] * edge, edge)
    acc[pl.ds(offset, edge), :] += term[...]

    @pl.when(step == pl.num_programs(0) - 1)
    def _():
        out_ref[...] = acc[...].astype(out_ref.dtype)


def accumulate(blocks, places, factors, mode, height):
    count, edge, _ = blocks.shape
    width = factors[0].shape[1]
    row_spec = lambda f: pl.BlockSpec((edge, width), lambda i, place: (place[i, f], 0))
    flops = 4 * count * edge**3 * width
    return pl.pallas_call(
        functools.partial(gradient_kernel, mode, 8),
        grid_spec=pltpu.PrefetchScalarGridSpec(
            num_scalar_prefetch=1,
            grid=(count,),
            in_specs=[
                pl.BlockSpec((1, edge, edge * edge), lambda i, place: (i, 0, 0)),
                row_spec(0),
                row_spec(1),
                row_spec(2),
            ],
            out_specs=pl.BlockSpec((height, width), lambda i, place: (0, 0)),
            scratch_shapes=[
                pltpu.VMEM((height, width), F32),
                pltpu.VMEM((edge, width), F32),
                pltpu.VMEM((2, 2 * edge, width), BF16),
            ],
        ),
        out_shape=jax.ShapeDtypeStruct((height, width), BF16),
        cost_estimate=pl.CostEstimate(flops=flops, bytes_accessed=2 * blocks.size, transcendentals=0),
        name=f"gradient{mode}",
    )(places, blocks, *factors)


def block_slots(coords, count, per_pair, held_rows):
    target = coords[:, 0] // held_rows
    same = target[:, None] == target[None, :]
    earlier = jnp.arange(count)[None, :] < jnp.arange(count)[:, None]
    before = jnp.sum((same & earlier).astype(jnp.int32), axis=1)
    return target * per_pair + before


def serve_rows(incoming, factor, edge, held_rows):
    width = factor.shape[1]
    within = incoming - lax.axis_index("ia") * held_rows
    safe_rows = jnp.clip(within, 0, held_rows - 1)
    picked = factor.astype(BF16).reshape(held_rows, edge, width)[safe_rows]
    return lax.all_to_all(picked, "ia", split_axis=0, concat_axis=0, tiled=True)


def per_device(blocks, coords, factor_one, factor_two, factor_three):
    count, edge, _ = blocks.shape
    groups = lax.axis_size("ia")
    span_one, width = factor_one.shape
    span_two = factor_two.shape[0]
    span_three = factor_three.shape[0]
    held_rows = span_one // edge
    per_pair = max(2, 2 * count // groups)
    slot = block_slots(coords, count, per_pair, held_rows)
    all_slots = groups * per_pair
    wanted = jnp.full((all_slots,), -1, jnp.int32).at[slot].set(coords[:, 0])
    incoming = lax.all_to_all(wanted, "ia", split_axis=0, concat_axis=0, tiled=True)
    fetched = serve_rows(incoming, factor_one, edge, held_rows).reshape(all_slots * edge, width)
    places = jnp.stack(
        [
            slot,
            coords[:, 1] - lax.axis_index("ja") * (span_two // edge),
            coords[:, 2] - lax.axis_index("ka") * (span_three // edge),
        ],
        axis=1,
    )
    slot_terms = accumulate(blocks, places, (fetched, factor_two, factor_three), 0, all_slots * edge)
    returned = lax.all_to_all(
        slot_terms.reshape(all_slots, edge, width), "ia", split_axis=0, concat_axis=0, tiled=True
    )
    within = incoming - lax.axis_index("ia") * held_rows
    selector = (within[None, :] == jnp.arange(held_rows)[:, None]).astype(BF16)
    first_part = jnp.dot(
        selector,
        returned.reshape(all_slots, edge * width),
        preferred_element_type=F32,
    ).reshape(span_one, width)
    first_part = lax.psum(first_part, ("ja", "ka"))
    factor_one = factor_one + STEP_SIZE * first_part
    first_rows = serve_rows(incoming, factor_one, edge, held_rows).reshape(all_slots * edge, width)
    second_part = accumulate(blocks, places, (first_rows, factor_two, factor_three), 1, span_two)
    factor_two = factor_two + STEP_SIZE * lax.psum(second_part.astype(F32), ("ia", "ka"))
    third_part = accumulate(blocks, places, (first_rows, factor_two, factor_three), 2, span_three)
    factor_three = factor_three + STEP_SIZE * lax.psum(third_part.astype(F32), ("ia", "ja"))
    return (factor_one, factor_two, factor_three)


def solution(mesh):
    in_specs = (
        P(("ia", "ja", "ka"), None, None),
        P(("ia", "ja", "ka"), None),
        P("ia", None),
        P("ja", None),
        P("ka", None),
    )
    out_specs = (P("ia", None), P("ja", None), P("ka", None))
    return jax.shard_map(
        per_device, mesh=mesh, in_specs=in_specs, out_specs=out_specs, check_vma=False
    )
```
